32 devices in a mesh: cuts: 4 (over z), tile: 8 (over y, x, core).
Axes of the slice: x: 2, y: 2, z: 4, core: 2. Of those that a mesh axis runs over, the one named last changes fastest.
Arguments:
- start_states: float32 [4, 3, 128, 2048], P('cuts', None, 'tile'), may hold values from -6 to 6
Outputs:
- next_states: float32 [4, 3, 128, 2048], P('cuts', None, 'tile')
The draws below stay inside these ranges and needn't reach their ends.
All inputs are finite; a program needn't handle non-finite values.
Results may differ from the reference program's by a relative error of at most 0.0001.
Values sent between devices are 32-bit elements; how exact they have to be, the bound alone decides.
A program may use at most 128 MiB of HBM per device.

```python
import jax
import jax.numpy as jnp
from jax import lax

NX = 2048
STEPS = 3
SLICES = 4
NY = 128
N_CUTS = 4


def level_of(stream_key, extent, shards, smallest, largest):
    gain = 1.0
    for axis_at, shards_of in shards:
        steps = jax.random.uniform(jax.random.fold_in(jax.random.fold_in(stream_key, 6), axis_at), (shards_of,), jnp.float32, smallest / len(shards), largest / len(shards))
        gain = gain * jnp.repeat(jnp.exp(steps), extent[axis_at] // shards_of).reshape((-1,) + (1,) * (len(extent) - 1 - axis_at))
    return gain


def centred(stream_key, extent, spread, limit, shards=(), dtype=jnp.bfloat16):
    result = jax.random.normal(stream_key, extent, jnp.float32) * spread
    if len(shards) > 0:
        result = level_of(stream_key, extent, shards, -0.22, 0.18) * result
    return jnp.clip(result, min=-limit, max=limit).astype(dtype)


def setup_inputs(seed: int = 0) -> dict:
    key_of = jax.random.split(jax.random.key(seed), 2)
    start_states = centred(key_of[0], (SLICES, 3, NY, NX), 1.0, 6.0, ((0, 4), (2, 8)), jnp.float32)
    return dict(start_states=start_states)


FINE_SPACING = 0.05
COARSE_SPACING = 0.1
FINE_STEP = 0.015
COARSE_STEP = 0.045

def depth_profile(columns, stride, length):
    centers = (jnp.arange(columns).astype(jnp.float32) + 0.5) * stride
    return 0.9 + 0.3 * jnp.sin(6.0 * jnp.pi * centers / length)

def along_x(values, spacing):
    padded = jnp.pad(values, [(0, 0)] * (values.ndim - 1) + [(1, 1)])
    return (padded[..., 2:] - padded[..., :-2]) / (2.0 * spacing)

def along_y(values, spacing):
    padded = jnp.pad(values, [(0, 0)] * (values.ndim - 2) + [(1, 1), (0, 0)])
    return (padded[..., 2:, :] - padded[..., :-2, :]) / (2.0 * spacing)

def second_y(values):
    padded = jnp.pad(values, [(0, 0)] * (values.ndim - 2) + [(1, 1), (0, 0)])
    return padded[..., 2:, :] - 2.0 * values + padded[..., :-2, :]

def solve_lines(forcing, seabed, spacing):
    columns = forcing.shape[-1]
    coupling = seabed * seabed / (3.0 * spacing * spacing)
    below_diag = (-coupling).at[0].set(0.0)
    above_diag = (-coupling).at[columns - 1].set(0.0)
    middle = 1.0 + 2.0 * coupling
    stacked_lines = forcing.reshape(-1, columns).T
    solved = lax.linalg.tridiagonal_solve(below_diag, middle, above_diag, stacked_lines)
    return solved.T.reshape(forcing.shape)

def wave_step(fields, seabed, spacing, time_step, inside):
    height = fields[..., 0, :, :]
    flux_x = fields[..., 1, :, :]
    flux_y = fields[..., 2, :, :]
    height_new = (height - time_step * (along_x(flux_x, spacing) + along_y(flux_y, spacing))) * inside
    forcing = jnp.stack([flux_x - time_step * seabed * along_x(height_new, spacing), flux_y - time_step * seabed * along_y(height_new, spacing)], axis=-3)
    trial_flux = solve_lines(forcing, seabed, spacing) * inside
    dispersion = seabed * seabed / 3.0
    weight = dispersion / (spacing * spacing + 4.0 * dispersion)
    fluxes = fields[..., 1:, :, :]
    fluxes_new = (trial_flux + weight * second_y(trial_flux - fluxes)) * inside
    return jnp.concatenate([height_new[..., None, :, :], fluxes_new], axis=-3)

def restrict(fields):
    shape_list = list(fields.shape)
    row_count = shape_list[-2]
    columns = shape_list[-1]
    blocks = fields.reshape(shape_list[:-2] + [row_count // 2, 2, columns // 2, 2])
    return 0.25 * jnp.sum(blocks, axis=(-3, -1))

def prolong(coarse):
    return jnp.repeat(jnp.repeat(coarse, 2, axis=-2), 2, axis=-1)

def reference(start_states):
    columns = start_states.shape[-1]
    fine_depth = depth_profile(columns, 1.0, columns)
    coarse_depth = depth_profile(columns // 2, 2.0, columns)
    fields = start_states
    for substep in range(STEPS):
        fields = wave_step(fields, fine_depth, FINE_SPACING, FINE_STEP, 1.0)
    fine_end = fields
    restricted_start = restrict(start_states)
    restricted_end = restrict(fine_end)
    previous = wave_step(restricted_start, coarse_depth, COARSE_SPACING, COARSE_STEP, 1.0)
    current = restricted_start[0]
    outputs = []
    for slice_index in range(N_CUTS):
        coarse_new = wave_step(current, coarse_depth, COARSE_SPACING, COARSE_STEP, 1.0) - previous[slice_index]
        outputs.append(prolong(coarse_new) + fine_end[slice_index])
        current = coarse_new + restricted_end[slice_index]
    return jnp.stack(outputs)
```

```python
import functools

import numpy as np
import jax
import jax.numpy as jnp
from jax import lax
from jax.experimental import pallas as pl
from jax.experimental.pallas import tpu as pltpu
from jax.sharding import PartitionSpec as P

STEPS = 3
FINE_SPACING = 0.05
COARSE_SPACING = 0.1
FINE_STEP = 0.015
COARSE_STEP = 0.045
LANES = 128
SUB = 8
MESH = pl.DeviceIdType.MESH
HIGHEST = lax.Precision.HIGHEST


def line_tables(tiles, fine_tiles, stride, length, spacing, step):
    groups = LANES // fine_tiles
    lane = np.arange(LANES)
    chunk = (lane % fine_tiles) * groups + lane // fine_tiles
    columns = tiles * LANES
    centers = (np.arange(columns) + 0.5) * stride
    depth = (0.9 + 0.3 * np.sin(6.0 * np.pi * centers / length)).reshape(LANES, tiles).T
    beta = depth * depth / 3.0
    b = beta / spacing**2
    mid = 1.0 + 2.0 * b
    last = tiles - 1
    inv = np.zeros_like(b)
    cp = np.zeros_like(b)
    for j in range(last):
        inv[j] = 1.0 / (mid[j] - (b[j] * cp[j - 1] if j else 0.0))
        cp[j] = b[j] * inv[j]
    run = np.ones_like(b)
    for j in range(1, tiles):
        run[j] = run[j - 1] * cp[j - 1]
    p = np.zeros_like(b)
    q = np.zeros_like(b)
    q[last] = 1.0
    for j in range(last - 1, -1, -1):
        p[j] = run[j + 1] + cp[j] * p[j + 1]
        q[j] = cp[j] * q[j + 1]
    system = np.zeros((LANES, LANES))
    for k in range(LANES):
        system[k, k] = mid[last, k] - b[last, k] * q[last - 1, k]
        if k:
            system[k, k - 1] = -b[last, k] * p[last - 1, k]
        if k + 1 < LANES:
            system[k, k] -= b[last, k] * p[0, k + 1]
            system[k, k + 1] = -b[last, k] * q[0, k + 1]
    solve = np.linalg.inv(system).T
    weights = np.zeros((2 * LANES, 2 * LANES))
    weights[:LANES, :LANES] = solve
    weights[LANES + 1 :, :LANES] = solve[:-1] * b[last, :-1, None]
    weights[:, LANES + 1 :] = weights[:, : LANES - 1]
    both = np.concatenate([chunk, LANES + chunk])
    weights = weights[both][:, both]
    slope = step * depth / (2.0 * spacing)
    weight = beta / (spacing**2 + 4.0 * beta)
    inv[last] = b[last]
    rows = np.stack([inv, cp, run, slope, weight])[:, :, chunk]
    return rows.astype(np.float32), weights.astype(np.float32)


def relaid(tiles):
    tiles = list(tiles)
    lane = lax.broadcasted_iota(jnp.int32, tiles[0].shape, 1)
    bit = 1
    while bit < len(tiles):
        keep = (lane & bit) == 0
        for t in range(len(tiles)):
            if t & bit == 0:
                a, b = tiles[t], tiles[t | bit]
                tiles[t] = jnp.where(keep, a, pltpu.roll(b, bit, 1))
                tiles[t | bit] = jnp.where(keep, pltpu.roll(a, LANES - bit, 1), b)
        bit *= 2
    return tiles


def wave(state, height, held, rows, weights, tiles, fine_tiles, factor, inside):
    count = state.shape[2]
    lane = lax.broadcasted_iota(jnp.int32, (count, LANES), 1)

    def chunk_before(x):
        wrapped = jnp.where(lane == 0, 0.0, pltpu.roll(x, fine_tiles + 1, 1))
        return jnp.where(lane >= fine_tiles, pltpu.roll(x, fine_tiles, 1), wrapped)

    def chunk_after(x):
        wrapped = jnp.where(lane == LANES - 1, 0.0, pltpu.roll(x, LANES - fine_tiles - 1, 1))
        return jnp.where(lane < LANES - fine_tiles, pltpu.roll(x, LANES - fine_tiles, 1), wrapped)

    def below(x):
        return pltpu.roll(x, count - 1, 0)

    def above(x):
        return pltpu.roll(x, 1, 0)

    def across(load, j):
        right = load(j + 1) if j + 1 < tiles else chunk_after(load(0))
        left = load(j - 1) if j else chunk_before(load(tiles - 1))
        return right - left

    def table(kind, j):
        return rows[kind, pl.ds(j, 1), :]

    for j in range(tiles):
        flux_y = state[2, j]
        spread = across(lambda i: state[1, i], j) + (below(flux_y) - above(flux_y))
        height[j] = (state[0, j] - factor * spread) * inside
    total = None
    inner = None
    for j in range(tiles):
        middle = height[j]
        slope = table(3, j)
        force_x = state[1, j] - slope * across(lambda i: height[i], j)
        force_y = state[2, j] - slope * (below(middle) - above(middle))
        force = jnp.concatenate([force_x, force_y], axis=0)
        if j == tiles - 1:
            edge = force + table(0, j) * inner
        elif j == 0:
            inner = force * table(0, j)
            total = inner
            held[j] = inner
        else:
            inner = force * table(0, j) + table(1, j) * inner
            total = total + table(2, j) * inner
            held[j] = inner
    met = jnp.dot(
        jnp.concatenate([edge, total], axis=1),
        weights[...],
        precision=HIGHEST,
        preferred_element_type=jnp.float32,
    )
    value = met[:, :LANES]
    before = met[:, LANES:]
    for j in range(tiles - 1, -1, -1):
        if j < tiles - 1:
            value = held[j] + table(2, j + 1) * before + table(1, j) * value
        weight = table(4, j)
        for part in range(2):
            trial = value[part * count : (part + 1) * count] * inside
            change = trial - state[1 + part, j]
            curve = below(change) - 2.0 * change + above(change)
            state[1 + part, j] = (trial + weight * curve) * inside
        state[0, j] = height[j]


def kernel(
    tile_count, slices, x_ref, fine_rows, fine_weights, coarse_rows, coarse_weights, out_ref,
    up_pair, up_y, down_pair, down_y, state, height, held,
    c_state, c_height, c_held, start, end, arrived, own, above_own, below_own, leaving,
    send, recv,
):
    cut = lax.axis_index("cuts")
    tile = lax.axis_index("tile")
    has_up = tile > 0
    has_down = tile < tile_count - 1
    planes, row_count, columns = x_ref.shape
    tiles = columns // LANES
    half = tiles // 2
    groups = row_count // SUB
    total_rows = row_count * tile_count

    barrier = pltpu.get_barrier_semaphore()
    near = [
        (has_up, {"tile": tile - 1}),
        (has_down, {"tile": tile + 1}),
        (cut > 0, {"cuts": cut - 1}),
        (cut < slices - 1, {"cuts": cut + 1}),
    ]
    for exists, place in near:
        @pl.when(exists)
        def _():
            pl.semaphore_signal(barrier, inc=1, device_id=place, device_id_type=MESH)
    pl.semaphore_wait(barrier, sum(exists.astype(jnp.int32) for exists, _ in near))

    def remote(source, target, which, place):
        return pltpu.make_async_remote_copy(
            src_ref=source, dst_ref=target, send_sem=send.at[which], recv_sem=recv.at[which],
            device_id=place, device_id_type=MESH,
        )

    to_up = {"tile": tile - 1}
    to_down = {"tile": tile + 1}
    two = pl.ds(0, 2)
    going_down = [
        remote(x_ref.at[two, pl.ds(row_count - SUB, SUB)], up_pair, 0, to_down),
        remote(x_ref.at[2, pl.ds(row_count - 2 * SUB, 2 * SUB)], up_y, 1, to_down),
    ]
    going_up = [
        remote(x_ref.at[two, pl.ds(0, SUB)], down_pair, 2, to_up),
        remote(x_ref.at[2, pl.ds(0, 2 * SUB)], down_y, 3, to_up),
    ]

    @pl.when(has_down)
    def _():
        for copy in going_down:
            copy.start()

    @pl.when(has_up)
    def _():
        for copy in going_up:
            copy.start()

    def place_rows(values, plane, row):
        parts = relaid([values[:, t * LANES : (t + 1) * LANES] for t in range(tiles)])
        for j in range(tiles):
            state[plane, j, pl.ds(row, SUB), :] = parts[j]

    tail = SUB * (groups + 2)
    for plane in range(planes):
        for group in range(groups):
            place_rows(x_ref[plane, pl.ds(group * SUB, SUB), :], plane, SUB * (group + 1))
    for plane in range(planes - 1):
        for j in range(tiles):
            state[plane, j, pl.ds(tail, SUB), :] = jnp.zeros((SUB, LANES), jnp.float32)

    def restrict(target):
        for plane in range(planes):
            for j in range(half):
                parts = [
                    state[plane, 2 * j + k, pl.ds(SUB + r, row_count // 2, stride=2), :]
                    for r in range(2)
                    for k in range(2)
                ]
                target[plane, j] = 0.25 * ((parts[0] + parts[1]) + (parts[2] + parts[3]))

    restrict(start)

    @pl.when(has_up)
    def _():
        for copy in going_down:
            copy.wait_recv()

    @pl.when(jnp.logical_not(has_up))
    def _():
        up_pair[...] = jnp.zeros_like(up_pair)
        up_y[...] = jnp.zeros_like(up_y)
        above_own[...] = jnp.zeros_like(above_own)

    @pl.when(has_down)
    def _():
        for copy in going_up:
            copy.wait_recv()

    @pl.when(jnp.logical_not(has_down))
    def _():
        down_pair[...] = jnp.zeros_like(down_pair)
        down_y[...] = jnp.zeros_like(down_y)
        below_own[...] = jnp.zeros_like(below_own)

    for plane in range(2):
        place_rows(up_pair[plane], plane, 0)
        place_rows(down_pair[plane], plane, tail - SUB)
    place_rows(up_y[pl.ds(SUB, SUB), :], 2, 0)
    place_rows(down_y[pl.ds(0, SUB), :], 2, tail - SUB)
    first = lax.broadcasted_iota(jnp.int32, (SUB, columns), 0) < SUB // 2
    mixed = jnp.where(first, down_y[pl.ds(SUB, SUB), :], up_y[pl.ds(0, SUB), :])
    place_rows(mixed, 2, tail)

    def mask(count, lead, total, origin):
        at = lax.broadcasted_iota(jnp.int32, (count, LANES), 0)
        row = jnp.where(at >= count - SUB // 2, at - count, at) - lead + origin
        return ((row >= 0) & (row < total)).astype(jnp.float32)

    fine_inside = mask(tail + SUB, SUB, total_rows, tile * row_count)

    def fine_step(step, carry):
        wave(
            state, height, held, fine_rows, fine_weights, tiles, tiles,
            FINE_STEP / (2.0 * FINE_SPACING), fine_inside,
        )
        return carry

    lax.fori_loop(0, STEPS, fine_step, 0)
    restrict(end)

    coarse_count = row_count // 2
    onward = remote(leaving, arrived, 4, {"cuts": cut + 1})
    own_down = remote(own, above_own, 5, to_down)
    own_up = remote(own, below_own, 6, to_up)

    @pl.when(cut == 0)
    def _():
        leaving[...] = end[...]

    @pl.when(cut > 0)
    def _():
        onward.wait_recv()
        own[...] = arrived[...] - start[...]

        @pl.when(has_down)
        def _():
            own_down.start()

        @pl.when(has_up)
        def _():
            own_up.start()

        @pl.when(has_up)
        def _():
            own_down.wait_recv()

        @pl.when(has_down)
        def _():
            own_up.wait_recv()

        near_rows = lax.broadcasted_iota(jnp.int32, (coarse_count, LANES), 0) < coarse_count // 2
        for plane in range(planes):
            for j in range(half):
                c_state[plane, j, pl.ds(0, coarse_count), :] = own[plane, j]
                c_state[plane, j, pl.ds(coarse_count, coarse_count), :] = jnp.where(
                    near_rows, below_own[plane, j], above_own[plane, j]
                )
        coarse_inside = mask(2 * coarse_count, 0, total_rows // 2, tile * coarse_count)
        wave(
            c_state, c_height, c_held, coarse_rows, coarse_weights, half, tiles,
            COARSE_STEP / (2.0 * COARSE_SPACING), coarse_inside,
        )
        for plane in range(planes):
            for j in range(half):
                leaving[plane, j] = c_state[plane, j, pl.ds(0, coarse_count), :] + end[plane, j]

    @pl.when(cut < slices - 1)
    def _():
        onward.start()

    @pl.when(cut > 0)
    def _():
        for plane in range(planes):
            for j in range(tiles):
                gain = c_state[plane, j // 2, pl.ds(0, coarse_count), :]
                for r in range(2):
                    at = pl.ds(SUB + r, coarse_count, stride=2)
                    state[plane, j, at, :] = state[plane, j, at, :] + gain

    for plane in range(planes):
        for group in range(groups):
            rows = pl.ds(SUB * (group + 1), SUB)
            parts = relaid([state[plane, j, rows, :] for j in range(tiles)])
            for t in range(tiles):
                out_ref[plane, pl.ds(group * SUB, SUB), pl.ds(t * LANES, LANES)] = parts[t]

    @pl.when(has_down)
    def _():
        for copy in going_down:
            copy.wait_send()

    @pl.when(has_up)
    def _():
        for copy in going_up:
            copy.wait_send()

    @pl.when(cut < slices - 1)
    def _():
        onward.wait_send()

    @pl.when((cut > 0) & has_down)
    def _():
        own_down.wait_send()

    @pl.when((cut > 0) & has_up)
    def _():
        own_up.wait_send()


def per_device(tile_count, slices, start_states):
    fields = start_states[0]
    planes, row_count, columns = fields.shape
    tiles = columns // LANES
    half = tiles // 2
    fine = line_tables(tiles, tiles, 1.0, columns, FINE_SPACING, FINE_STEP)
    coarse = line_tables(half, tiles, 2.0, columns, COARSE_SPACING, COARSE_STEP)
    fine_count = row_count + 3 * SUB
    coarse_count = row_count // 2
    f32 = jnp.float32
    slab = pltpu.VMEM((planes, half, coarse_count, LANES), f32)
    out = pl.pallas_call(
        functools.partial(kernel, tile_count, slices),
        out_shape=jax.ShapeDtypeStruct(fields.shape, f32),
        in_specs=[pl.BlockSpec(memory_space=pltpu.VMEM)] * 5,
        out_specs=pl.BlockSpec(memory_space=pltpu.VMEM),
        scratch_shapes=[
            pltpu.VMEM((2, SUB, columns), f32),
            pltpu.VMEM((2 * SUB, columns), f32),
            pltpu.VMEM((2, SUB, columns), f32),
            pltpu.VMEM((2 * SUB, columns), f32),
            pltpu.VMEM((planes, tiles, fine_count, LANES), f32),
            pltpu.VMEM((tiles, fine_count, LANES), f32),
            pltpu.VMEM((tiles, 2 * fine_count, LANES), f32),
            pltpu.VMEM((planes, half, 2 * coarse_count, LANES), f32),
            pltpu.VMEM((half, 2 * coarse_count, LANES), f32),
            pltpu.VMEM((half, 4 * coarse_count, LANES), f32),
        ]
        + [slab] * 7
        + [pltpu.SemaphoreType.DMA((7,)), pltpu.SemaphoreType.DMA((7,))],
        compiler_params=pltpu.CompilerParams(collective_id=0, has_side_effects=True),
    )(fields, *[jnp.asarray(a) for a in fine + coarse])
    return out[None]


def solution(mesh):
    spec = P("cuts", None, "tile", None)
    body = functools.partial(per_device, mesh.shape["tile"], mesh.shape["cuts"])
    return jax.shard_map(body, mesh=mesh, in_specs=(spec,), out_specs=spec, check_vma=False)
```

```python
import functools

import numpy as np
import jax
import jax.numpy as jnp
from jax import lax
from jax.experimental import pallas as pl
from jax.experimental.pallas import tpu as pltpu
from jax.sharding import PartitionSpec as P

STEPS = 3
FINE_SPACING = 0.05
COARSE_SPACING = 0.1
FINE_STEP = 0.015
COARSE_STEP = 0.045
LANES = 128
SUB = 8
HALO = 3
MESH = pl.DeviceIdType.MESH
HIGHEST = lax.Precision.HIGHEST


def line_tables(tiles, fine_tiles, stride, length, spacing, step):
    groups = LANES // fine_tiles
    lane = np.arange(LANES)
    chunk = (lane % fine_tiles) * groups + lane // fine_tiles
    columns = tiles * LANES
    centers = (np.arange(columns) + 0.5) * stride
    depth = (0.9 + 0.3 * np.sin(6.0 * np.pi * centers / length)).reshape(LANES, tiles).T
    beta = depth * depth / 3.0
    b = beta / spacing**2
    mid = 1.0 + 2.0 * b
    last = tiles - 1
    inv = np.zeros_like(b)
    cp = np.zeros_like(b)
    for j in range(last):
        inv[j] = 1.0 / (mid[j] - (b[j] * cp[j - 1] if j else 0.0))
        cp[j] = b[j] * inv[j]
    run = np.ones_like(b)
    for j in range(1, tiles):
        run[j] = run[j - 1] * cp[j - 1]
    p = np.zeros_like(b)
    q = np.zeros_like(b)
    q[last] = 1.0
    for j in range(last - 1, -1, -1):
        p[j] = run[j + 1] + cp[j] * p[j + 1]
        q[j] = cp[j] * q[j + 1]
    system = np.zeros((LANES, LANES))
    for k in range(LANES):
        system[k, k] = mid[last, k] - b[last, k] * q[last - 1, k]
        if k:
            system[k, k - 1] = -b[last, k] * p[last - 1, k]
        if k + 1 < LANES:
            system[k, k] -= b[last, k] * p[0, k + 1]
            system[k, k + 1] = -b[last, k] * q[0, k + 1]
    solve = np.linalg.inv(system).T
    weights = np.zeros((2 * LANES, 2 * LANES))
    weights[:LANES, :LANES] = solve
    weights[LANES + 1 :, :LANES] = solve[:-1] * b[last, :-1, None]
    weights[:, LANES + 1 :] = weights[:, : LANES - 1]
    both = np.concatenate([chunk, LANES + chunk])
    weights = weights[both][:, both]
    slope = step * depth / (2.0 * spacing)
    weight = beta / (spacing**2 + 4.0 * beta)
    inv[last] = b[last]
    rows = np.stack([inv, cp, run, slope, weight])[:, :, chunk]
    return rows.astype(np.float32), weights.astype(np.float32)


def relaid(tiles):
    tiles = list(tiles)
    lane = lax.broadcasted_iota(jnp.int32, tiles[0].shape, 1)
    bit = 1
    while bit < len(tiles):
        keep = (lane & bit) == 0
        for t in range(len(tiles)):
            if t & bit == 0:
                a, b = tiles[t], tiles[t | bit]
                tiles[t] = jnp.where(keep, a, pltpu.roll(b, bit, 1))
                tiles[t | bit] = jnp.where(keep, pltpu.roll(a, LANES - bit, 1), b)
        bit *= 2
    return tiles


def wave(state, height, held, rows, weights, tiles, fine_tiles, factor, inside):
    count = state.shape[2]
    lane = lax.broadcasted_iota(jnp.int32, (count, LANES), 1)

    def chunk_before(x):
        wrapped = jnp.where(lane == 0, 0.0, pltpu.roll(x, fine_tiles + 1, 1))
        return jnp.where(lane >= fine_tiles, pltpu.roll(x, fine_tiles, 1), wrapped)

    def chunk_after(x):
        wrapped = jnp.where(lane == LANES - 1, 0.0, pltpu.roll(x, LANES - fine_tiles - 1, 1))
        return jnp.where(lane < LANES - fine_tiles, pltpu.roll(x, LANES - fine_tiles, 1), wrapped)

    def below(x):
        return pltpu.roll(x, count - 1, 0)

    def above(x):
        return pltpu.roll(x, 1, 0)

    def across(load, j):
        right = load(j + 1) if j + 1 < tiles else chunk_after(load(0))
        left = load(j - 1) if j else chunk_before(load(tiles - 1))
        return right - left

    def table(kind, j):
        return rows[kind, pl.ds(j, 1), :]

    for j in range(tiles):
        flux_y = state[2, j]
        spread = across(lambda i: state[1, i], j) + (below(flux_y) - above(flux_y))
        height[j] = (state[0, j] - factor * spread) * inside
    total = None
    inner = None
    for j in range(tiles):
        middle = height[j]
        slope = table(3, j)
        force_x = state[1, j] - slope * across(lambda i: height[i], j)
        force_y = state[2, j] - slope * (below(middle) - above(middle))
        force = jnp.concatenate([force_x, force_y], axis=0)
        if j == tiles - 1:
            edge = force + table(0, j) * inner
        elif j == 0:
            inner = force * table(0, j)
            total = inner
            held[j] = inner
        else:
            inner = force * table(0, j) + table(1, j) * inner
            total = total + table(2, j) * inner
            held[j] = inner
    met = jnp.dot(
        jnp.concatenate([edge, total], axis=1),
        weights[...],
        precision=HIGHEST,
        preferred_element_type=jnp.float32,
    )
    value = met[:, :LANES]
    before = met[:, LANES:]
    for j in range(tiles - 1, -1, -1):
        if j < tiles - 1:
            value = held[j] + table(2, j + 1) * before + table(1, j) * value
        weight = table(4, j)
        for part in range(2):
            trial = value[part * count : (part + 1) * count] * inside
            change = trial - state[1 + part, j]
            curve = below(change) - 2.0 * change + above(change)
            state[1 + part, j] = (trial + weight * curve) * inside
        state[0, j] = height[j]


def kernel(
    tile_count, slices, x_hbm, fine_rows_hbm, fine_weights_hbm, coarse_rows_hbm,
    coarse_weights_hbm, out_ref,
    x_ref, fine_rows, fine_weights, coarse_rows, coarse_weights,
    up_main, down_main, edge, up_edge, down_edge, state, height, held,
    c_state, c_height, c_held, start, end, arrived, leaving, low, far_start, above_in, below_in,
    local, send, recv,
):
    cut = lax.axis_index("cuts")
    tile = lax.axis_index("tile")
    has_up = tile > 0
    has_down = tile < tile_count - 1
    has_before = cut > 0
    has_after = cut < slices - 1
    planes, row_count, columns = x_ref.shape
    tiles = columns // LANES
    half = tiles // 2
    groups = row_count // SUB
    total_rows = row_count * tile_count
    coarse_count = row_count // 2

    pairs = [
        (x_hbm, x_ref), (fine_rows_hbm, fine_rows), (fine_weights_hbm, fine_weights),
        (coarse_rows_hbm, coarse_rows), (coarse_weights_hbm, coarse_weights),
    ]
    loads = [pltpu.make_async_copy(a, b, local.at[i]) for i, (a, b) in enumerate(pairs)]
    for load in loads:
        load.start()

    barrier = pltpu.get_barrier_semaphore()
    near = [(has_up, cut, tile - 1), (has_down, cut, tile + 1)]
    for there, other in ((has_before, cut - 1), (has_after, cut + 1)):
        near.append((there, other, tile))
        near.append((there & has_up, other, tile - 1))
        near.append((there & has_down, other, tile + 1))
    for exists, to_cut, to_tile in near:
        @pl.when(exists)
        def _():
            pl.semaphore_signal(
                barrier, inc=1, device_id=(to_cut, to_tile), device_id_type=MESH
            )
    pl.semaphore_wait(barrier, sum(exists.astype(jnp.int32) for exists, _, _ in near))

    def remote(source, target, which, to_cut, to_tile):
        return pltpu.make_async_remote_copy(
            src_ref=source, dst_ref=target, send_sem=send.at[which], recv_sem=recv.at[which],
            device_id=(to_cut, to_tile), device_id_type=MESH,
        )

    one = pl.ds(0, 1)
    main_down = remote(
        x_hbm.at[:, pl.ds(row_count - SUB, SUB)], up_main, 0, cut, tile + 1
    )
    edge_down = remote(edge.at[one], up_edge.at[one], 1, cut, tile + 1)
    main_up = remote(x_hbm.at[:, pl.ds(0, SUB)], down_main, 2, cut, tile - 1)
    edge_up = remote(x_hbm.at[planes - 1, pl.ds(SUB, 1)], down_edge.at[one], 3, cut, tile - 1)

    @pl.when(has_down)
    def _():
        main_down.start()

    @pl.when(has_up)
    def _():
        edge_up.start()
        main_up.start()

    loads[0].wait()
    edge[one, :] = x_ref[planes - 1, pl.ds(row_count - SUB - 1, 1), :]

    def place_rows(values, plane, row):
        parts = relaid([values[:, t * LANES : (t + 1) * LANES] for t in range(tiles)])
        for j in range(tiles):
            state[plane, j, pl.ds(row, SUB), :] = parts[j]

    tail = SUB * (groups + 2)
    for plane in range(planes - 1):
        for group in range(groups):
            place_rows(x_ref[plane, pl.ds(group * SUB, SUB), :], plane, SUB * (group + 1))
        for j in range(tiles):
            state[plane, j, pl.ds(tail, SUB), :] = jnp.zeros((SUB, LANES), jnp.float32)

    @pl.when(has_down)
    def _():
        edge_down.start()

    for group in range(groups):
        place_rows(
            x_ref[planes - 1, pl.ds(group * SUB, SUB), :], planes - 1, SUB * (group + 1)
        )

    def restricted(plane, j, row, count):
        parts = [
            state[plane, 2 * j + k, pl.ds(row + r, count, stride=2), :]
            for r in range(2)
            for k in range(2)
        ]
        return 0.25 * ((parts[0] + parts[1]) + (parts[2] + parts[3]))

    def each_slab():
        return [(plane, j) for plane in range(planes) for j in range(half)]

    for plane, j in each_slab():
        start[plane, j] = restricted(plane, j, SUB, coarse_count)
    for load in loads[1:]:
        load.wait()

    @pl.when(jnp.logical_not(has_up))
    def _():
        up_main[...] = jnp.zeros_like(up_main)
        up_edge[...] = jnp.zeros_like(up_edge)

    @pl.when(jnp.logical_not(has_down))
    def _():
        down_main[...] = jnp.zeros_like(down_main)
        down_edge[...] = jnp.zeros_like(down_edge)

    @pl.when(has_up)
    def _():
        main_down.wait_recv()
        edge_down.wait_recv()

    @pl.when(has_down)
    def _():
        main_up.wait_recv()
        edge_up.wait_recv()

    for plane in range(planes):
        place_rows(up_main[plane], plane, 0)
        place_rows(down_main[plane], plane, tail - SUB)
    at_row = lax.broadcasted_iota(jnp.int32, (SUB, columns), 0)
    mixed = jnp.where(
        at_row == 0,
        jnp.broadcast_to(down_edge[one, :], (SUB, columns)),
        jnp.where(
            at_row == SUB - 1, jnp.broadcast_to(up_edge[one, :], (SUB, columns)), 0.0
        ),
    )
    place_rows(mixed, planes - 1, tail)

    for plane, j in each_slab():
        far_start[plane, j, pl.ds(0, SUB // 2), :] = restricted(plane, j, tail - SUB, SUB // 2)
        far_start[plane, j, pl.ds(SUB // 2, SUB // 2), :] = restricted(plane, j, 0, SUB // 2)

    def mask(count, lead, total, origin):
        at = lax.broadcasted_iota(jnp.int32, (count, LANES), 0)
        row = jnp.where(at >= count - SUB // 2, at - count, at) - lead + origin
        return ((row >= 0) & (row < total)).astype(jnp.float32)

    fine_inside = mask(tail + SUB, SUB, total_rows, tile * row_count)

    def fine_step(step, carry):
        wave(
            state, height, held, fine_rows, fine_weights, tiles, tiles,
            FINE_STEP / (2.0 * FINE_SPACING), fine_inside,
        )
        return carry

    lax.fori_loop(0, STEPS, fine_step, 0)

    three = pl.ds(0, HALO)
    part = (slice(None), slice(None), three)
    to_own = remote(leaving, arrived, 4, cut + 1, tile)
    to_above = remote(leaving.at[part], below_in.at[part], 5, cut + 1, tile - 1)
    to_below = remote(low.at[part], above_in.at[part], 6, cut + 1, tile + 1)

    def leave(plane, j, value):
        leaving[plane, j] = value
        low[plane, j] = pltpu.roll(value, HALO, 0)

    @pl.when(cut == 0)
    def _():
        for plane, j in each_slab():
            leave(plane, j, restricted(plane, j, SUB, coarse_count))

    @pl.when(has_before)
    def _():
        for plane, j in each_slab():
            end[plane, j] = restricted(plane, j, SUB, coarse_count)

        @pl.when(jnp.logical_not(has_up))
        def _():
            above_in[...] = jnp.zeros_like(above_in)

        @pl.when(jnp.logical_not(has_down))
        def _():
            below_in[...] = jnp.zeros_like(below_in)

        @pl.when(has_up)
        def _():
            to_below.wait_recv()

        @pl.when(has_down)
        def _():
            to_above.wait_recv()

        at = lax.broadcasted_iota(jnp.int32, (SUB, LANES), 0)
        for plane, j in each_slab():
            around = jnp.where(
                at < HALO,
                below_in[plane, j],
                jnp.where(
                    at >= SUB - HALO, pltpu.roll(above_in[plane, j], SUB - HALO, 0), 0.0
                ),
            )
            c_state[plane, j, pl.ds(coarse_count, SUB), :] = around - far_start[plane, j]
        to_own.wait_recv()
        for plane, j in each_slab():
            c_state[plane, j, pl.ds(0, coarse_count), :] = arrived[plane, j] - start[plane, j]
        coarse_inside = mask(coarse_count + SUB, 0, total_rows // 2, tile * coarse_count)
        wave(
            c_state, c_height, c_held, coarse_rows, coarse_weights, half, tiles,
            COARSE_STEP / (2.0 * COARSE_SPACING), coarse_inside,
        )
        for plane, j in each_slab():
            leave(plane, j, c_state[plane, j, pl.ds(0, coarse_count), :] + end[plane, j])

    @pl.when(has_after & has_up)
    def _():
        to_above.start()

    @pl.when(has_after & has_down)
    def _():
        to_below.start()

    @pl.when(has_after)
    def _():
        to_own.start()

    @pl.when(has_before)
    def _():
        for plane in range(planes):
            for j in range(tiles):
                gain = c_state[plane, j // 2, pl.ds(0, coarse_count), :]
                for r in range(2):
                    at = pl.ds(SUB + r, coarse_count, stride=2)
                    state[plane, j, at, :] = state[plane, j, at, :] + gain

    for plane in range(planes):
        for group in range(groups):
            rows = pl.ds(SUB * (group + 1), SUB)
            parts = relaid([state[plane, j, rows, :] for j in range(tiles)])
            for t in range(tiles):
                out_ref[plane, pl.ds(group * SUB, SUB), pl.ds(t * LANES, LANES)] = parts[t]

    @pl.when(has_down)
    def _():
        main_down.wait_send()
        edge_down.wait_send()

    @pl.when(has_up)
    def _():
        main_up.wait_send()
        edge_up.wait_send()

    @pl.when(has_after & has_up)
    def _():
        to_above.wait_send()

    @pl.when(has_after & has_down)
    def _():
        to_below.wait_send()

    @pl.when(has_after)
    def _():
        to_own.wait_send()


def per_device(tile_count, slices, start_states):
    fields = start_states[0]
    planes, row_count, columns = fields.shape
    tiles = columns // LANES
    half = tiles // 2
    fine = line_tables(tiles, tiles, 1.0, columns, FINE_SPACING, FINE_STEP)
    coarse = line_tables(half, tiles, 2.0, columns, COARSE_SPACING, COARSE_STEP)
    fine_count = row_count + 3 * SUB
    coarse_count = row_count // 2
    f32 = jnp.float32
    slab = pltpu.VMEM((planes, half, coarse_count, LANES), f32)
    out = pl.pallas_call(
        functools.partial(kernel, tile_count, slices),
        out_shape=jax.ShapeDtypeStruct(fields.shape, f32),
        in_specs=[pl.BlockSpec(memory_space=pl.ANY)] * 5,
        out_specs=pl.BlockSpec(memory_space=pltpu.VMEM),
        scratch_shapes=[pltpu.VMEM(fields.shape, f32)]
        + [pltpu.VMEM(a.shape, f32) for a in fine + coarse]
        + [pltpu.VMEM((planes, SUB, columns), f32)] * 2
        + [pltpu.VMEM((SUB, columns), f32)] * 3
        + [
            pltpu.VMEM((planes, tiles, fine_count, LANES), f32),
            pltpu.VMEM((tiles, fine_count, LANES), f32),
            pltpu.VMEM((tiles, 2 * fine_count, LANES), f32),
            pltpu.VMEM((planes, half, 2 * coarse_count, LANES), f32),
            pltpu.VMEM((half, 2 * coarse_count, LANES), f32),
            pltpu.VMEM((half, 4 * coarse_count, LANES), f32),
        ]
        + [slab] * 8
        + [
            pltpu.SemaphoreType.DMA((5,)),
            pltpu.SemaphoreType.DMA((7,)),
            pltpu.SemaphoreType.DMA((7,)),
        ],
        compiler_params=pltpu.CompilerParams(collective_id=0, has_side_effects=True),
    )(fields, *[jnp.asarray(a) for a in fine + coarse])
    return out[None]


def solution(mesh):
    spec = P("cuts", None, "tile", None)
    body = functools.partial(per_device, mesh.shape["tile"], mesh.shape["cuts"])
    return jax.shard_map(body, mesh=mesh, in_specs=(spec,), out_specs=spec, check_vma=False)
```

```python
import functools

import numpy as np
import jax
import jax.numpy as jnp
from jax import lax
from jax.experimental import pallas as pl
from jax.experimental.pallas import tpu as pltpu
from jax.sharding import PartitionSpec as P

STEPS = 3
FINE_SPACING = 0.05
COARSE_SPACING = 0.1
FINE_STEP = 0.015
COARSE_STEP = 0.045
LANES = 128
SUB = 8
HALO = (2, 2, 3)
MESH = pl.DeviceIdType.MESH
HIGH = lax.Precision.HIGH


def line_tables(tiles, fine_tiles, stride, length, spacing, step):
    groups = LANES // fine_tiles
    lane = np.arange(LANES)
    chunk = (lane % fine_tiles) * groups + lane // fine_tiles
    columns = tiles * LANES
    centers = (np.arange(columns) + 0.5) * stride
    depth = (0.9 + 0.3 * np.sin(6.0 * np.pi * centers / length)).reshape(LANES, tiles).T
    beta = depth * depth / 3.0
    b = beta / spacing**2
    mid = 1.0 + 2.0 * b
    last = tiles - 1
    inv = np.zeros_like(b)
    cp = np.zeros_like(b)
    for j in range(last):
        inv[j] = 1.0 / (mid[j] - (b[j] * cp[j - 1] if j else 0.0))
        cp[j] = b[j] * inv[j]
    run = np.ones_like(b)
    for j in range(1, tiles):
        run[j] = run[j - 1] * cp[j - 1]
    p = np.zeros_like(b)
    q = np.zeros_like(b)
    q[last] = 1.0
    for j in range(last - 1, -1, -1):
        p[j] = run[j + 1] + cp[j] * p[j + 1]
        q[j] = cp[j] * q[j + 1]
    system = np.zeros((LANES, LANES))
    for k in range(LANES):
        system[k, k] = mid[last, k] - b[last, k] * q[last - 1, k]
        if k:
            system[k, k - 1] = -b[last, k] * p[last - 1, k]
        if k + 1 < LANES:
            system[k, k] -= b[last, k] * p[0, k + 1]
            system[k, k + 1] = -b[last, k] * q[0, k + 1]
    solve = np.linalg.inv(system).T
    weights = np.zeros((2 * LANES, 2 * LANES))
    weights[:LANES, :LANES] = solve
    weights[LANES + 1 :, :LANES] = solve[:-1] * b[last, :-1, None]
    weights[:, LANES + 1 :] = weights[:, : LANES - 1]
    both = np.concatenate([chunk, LANES + chunk])
    weights = weights[both][:, both]
    slope = step * depth / (2.0 * spacing)
    weight = beta / (spacing**2 + 4.0 * beta)
    inv[last] = b[last]
    rows = np.stack([inv, cp, run, slope, weight])[:, :, chunk]
    return rows.astype(np.float32), weights.astype(np.float32)


def relaid(tiles):
    tiles = list(tiles)
    lane = lax.broadcasted_iota(jnp.int32, tiles[0].shape, 1)
    bit = 1
    while bit < len(tiles):
        keep = (lane & bit) == 0
        for t in range(len(tiles)):
            if t & bit == 0:
                a, b = tiles[t], tiles[t | bit]
                tiles[t] = jnp.where(keep, a, pltpu.roll(b, bit, 1))
                tiles[t | bit] = jnp.where(keep, pltpu.roll(a, LANES - bit, 1), b)
        bit *= 2
    return tiles


def wave(state, height, held, rows, weights, tiles, fine_tiles, factor, inside):
    count = state.shape[2]
    lane = lax.broadcasted_iota(jnp.int32, (count, LANES), 1)

    def chunk_before(x):
        wrapped = jnp.where(lane == 0, 0.0, pltpu.roll(x, fine_tiles + 1, 1))
        return jnp.where(lane >= fine_tiles, pltpu.roll(x, fine_tiles, 1), wrapped)

    def chunk_after(x):
        wrapped = jnp.where(lane == LANES - 1, 0.0, pltpu.roll(x, LANES - fine_tiles - 1, 1))
        return jnp.where(lane < LANES - fine_tiles, pltpu.roll(x, LANES - fine_tiles, 1), wrapped)

    def below(x):
        return pltpu.roll(x, count - 1, 0)

    def above(x):
        return pltpu.roll(x, 1, 0)

    def across(load, j):
        right = load(j + 1) if j + 1 < tiles else chunk_after(load(0))
        left = load(j - 1) if j else chunk_before(load(tiles - 1))
        return right - left

    def table(kind, j):
        return rows[kind, pl.ds(j, 1), :]

    for j in range(tiles):
        flux_y = state[2, j]
        spread = across(lambda i: state[1, i], j) + (below(flux_y) - above(flux_y))
        height[j] = (state[0, j] - factor * spread) * inside
    total = None
    inner = None
    for j in range(tiles):
        middle = height[j]
        slope = table(3, j)
        force_x = state[1, j] - slope * across(lambda i: height[i], j)
        force_y = state[2, j] - slope * (below(middle) - above(middle))
        force = jnp.concatenate([force_x, force_y], axis=0)
        if j == tiles - 1:
            edge = force + table(0, j) * inner
        elif j == 0:
            inner = force * table(0, j)
            total = inner
            held[j] = inner
        else:
            inner = force * table(0, j) + table(1, j) * inner
            total = total + table(2, j) * inner
            held[j] = inner
    met = jnp.dot(
        jnp.concatenate([edge, total], axis=1),
        weights[...],
        precision=HIGH,
        preferred_element_type=jnp.float32,
    )
    value = met[:, :LANES]
    before = met[:, LANES:]
    for j in range(tiles - 1, -1, -1):
        if j < tiles - 1:
            value = held[j] + table(2, j + 1) * before + table(1, j) * value
        weight = table(4, j)
        for part in range(2):
            trial = value[part * count : (part + 1) * count] * inside
            change = trial - state[1 + part, j]
            curve = below(change) - 2.0 * change + above(change)
            state[1 + part, j] = (trial + weight * curve) * inside
        state[0, j] = height[j]


def kernel(
    tile_count, slices, x_hbm, fine_rows_hbm, fine_weights_hbm, coarse_rows_hbm,
    coarse_weights_hbm, fine_hbm, gain_ref,
    natural, x_ref, fine_rows, fine_weights, coarse_rows, coarse_weights,
    up_main, down_main, edge, up_edge, down_edge, state, height, held,
    c_state, c_height, c_held, start, end, arrived, leaving, low, far_start, above_in, below_in,
    local, send, recv,
):
    cut = lax.axis_index("cuts")
    tile = lax.axis_index("tile")
    has_up = tile > 0
    has_down = tile < tile_count - 1
    has_before = cut > 0
    has_after = cut < slices - 1
    planes, row_count, columns = x_ref.shape
    tiles = columns // LANES
    half = tiles // 2
    groups = row_count // SUB
    total_rows = row_count * tile_count
    coarse_count = row_count // 2

    pairs = [
        (x_hbm, x_ref), (fine_rows_hbm, fine_rows), (fine_weights_hbm, fine_weights),
        (coarse_rows_hbm, coarse_rows), (coarse_weights_hbm, coarse_weights),
    ]
    loads = [pltpu.make_async_copy(a, b, local.at[i]) for i, (a, b) in enumerate(pairs)]
    for load in loads:
        load.start()

    barrier = pltpu.get_barrier_semaphore()
    near = [(has_up, cut, tile - 1), (has_down, cut, tile + 1)]
    for there, other in ((has_before, cut - 1), (has_after, cut + 1)):
        near.append((there, other, tile))
        near.append((there & has_up, other, tile - 1))
        near.append((there & has_down, other, tile + 1))
    for exists, to_cut, to_tile in near:
        @pl.when(exists)
        def _():
            pl.semaphore_signal(
                barrier, inc=1, device_id=(to_cut, to_tile), device_id_type=MESH
            )
    pl.semaphore_wait(barrier, sum(exists.astype(jnp.int32) for exists, _, _ in near))

    def remote(source, target, which, to_cut, to_tile):
        return pltpu.make_async_remote_copy(
            src_ref=source, dst_ref=target, send_sem=send.at[which], recv_sem=recv.at[which],
            device_id=(to_cut, to_tile), device_id_type=MESH,
        )

    one = pl.ds(0, 1)
    main_down = remote(
        x_hbm.at[:, pl.ds(row_count - SUB, SUB)], up_main, 0, cut, tile + 1
    )
    edge_down = remote(edge.at[one], up_edge.at[one], 1, cut, tile + 1)
    main_up = remote(x_hbm.at[:, pl.ds(0, SUB)], down_main, 2, cut, tile - 1)
    edge_up = remote(x_hbm.at[planes - 1, pl.ds(SUB, 1)], down_edge.at[one], 3, cut, tile - 1)

    @pl.when(has_down)
    def _():
        main_down.start()

    @pl.when(has_up)
    def _():
        edge_up.start()
        main_up.start()

    loads[0].wait()
    edge[one, :] = x_ref[planes - 1, pl.ds(row_count - SUB - 1, 1), :]

    def place_rows(values, plane, row):
        parts = relaid([values[:, t * LANES : (t + 1) * LANES] for t in range(tiles)])
        for j in range(tiles):
            state[plane, j, pl.ds(row, SUB), :] = parts[j]

    tail = SUB * (groups + 2)
    for plane in range(planes - 1):
        for group in range(groups):
            place_rows(x_ref[plane, pl.ds(group * SUB, SUB), :], plane, SUB * (group + 1))
        for j in range(tiles):
            state[plane, j, pl.ds(tail, SUB), :] = jnp.zeros((SUB, LANES), jnp.float32)

    @pl.when(has_down)
    def _():
        edge_down.start()

    for group in range(groups):
        place_rows(
            x_ref[planes - 1, pl.ds(group * SUB, SUB), :], planes - 1, SUB * (group + 1)
        )

    def restricted(plane, j, row, count):
        parts = [
            state[plane, 2 * j + k, pl.ds(row + r, count, stride=2), :]
            for r in range(2)
            for k in range(2)
        ]
        return 0.25 * ((parts[0] + parts[1]) + (parts[2] + parts[3]))

    def each_slab():
        return [(plane, j) for plane in range(planes) for j in range(half)]

    for plane, j in each_slab():
        start[plane, j] = restricted(plane, j, SUB, coarse_count)
    for load in loads[1:]:
        load.wait()

    @pl.when(jnp.logical_not(has_up))
    def _():
        up_main[...] = jnp.zeros_like(up_main)
        up_edge[...] = jnp.zeros_like(up_edge)

    @pl.when(jnp.logical_not(has_down))
    def _():
        down_main[...] = jnp.zeros_like(down_main)
        down_edge[...] = jnp.zeros_like(down_edge)

    @pl.when(has_up)
    def _():
        main_down.wait_recv()
        edge_down.wait_recv()

    @pl.when(has_down)
    def _():
        main_up.wait_recv()
        edge_up.wait_recv()

    for plane in range(planes):
        place_rows(up_main[plane], plane, 0)
        place_rows(down_main[plane], plane, tail - SUB)
    at_row = lax.broadcasted_iota(jnp.int32, (SUB, columns), 0)
    mixed = jnp.where(
        at_row == 0,
        jnp.broadcast_to(down_edge[one, :], (SUB, columns)),
        jnp.where(
            at_row == SUB - 1, jnp.broadcast_to(up_edge[one, :], (SUB, columns)), 0.0
        ),
    )
    place_rows(mixed, planes - 1, tail)

    for plane, j in each_slab():
        far_start[plane, j, pl.ds(0, SUB // 2), :] = restricted(plane, j, tail - SUB, SUB // 2)
        far_start[plane, j, pl.ds(SUB // 2, SUB // 2), :] = restricted(plane, j, 0, SUB // 2)

    def mask(count, lead, total, origin):
        at = lax.broadcasted_iota(jnp.int32, (count, LANES), 0)
        row = jnp.where(at >= count - SUB // 2, at - count, at) - lead + origin
        return ((row >= 0) & (row < total)).astype(jnp.float32)

    fine_inside = mask(tail + SUB, SUB, total_rows, tile * row_count)

    def fine_step(step, carry):
        wave(
            state, height, held, fine_rows, fine_weights, tiles, tiles,
            FINE_STEP / (2.0 * FINE_SPACING), fine_inside,
        )
        return carry

    lax.fori_loop(0, STEPS, fine_step, 0)

    last = planes - 1
    first_part = (pl.ds(0, last), slice(None), pl.ds(0, HALO[0]))
    last_part = (last, slice(None), pl.ds(0, HALO[last]))
    to_own = remote(leaving, arrived, 4, cut + 1, tile)
    to_above = [
        remote(leaving.at[part], below_in.at[part], 5 + i, cut + 1, tile - 1)
        for i, part in enumerate((first_part, last_part))
    ]
    to_below = [
        remote(low.at[part], above_in.at[part], 7 + i, cut + 1, tile + 1)
        for i, part in enumerate((first_part, last_part))
    ]

    def leave(plane, j, value):
        leaving[plane, j] = value
        low[plane, j] = pltpu.roll(value, HALO[plane], 0)

    def launch():
        @pl.when(has_after & has_up)
        def _():
            for copy in to_above:
                copy.start()

        @pl.when(has_after & has_down)
        def _():
            for copy in to_below:
                copy.start()

        @pl.when(has_after)
        def _():
            to_own.start()

    @pl.when(cut == 0)
    def _():
        for plane, j in each_slab():
            leave(plane, j, restricted(plane, j, SUB, coarse_count))
        launch()
        gain_ref[...] = jnp.zeros_like(gain_ref)

    for plane in range(planes):
        for group in range(groups):
            rows = pl.ds(SUB * (group + 1), SUB)
            parts = relaid([state[plane, j, rows, :] for j in range(tiles)])
            for t in range(tiles):
                natural[plane, pl.ds(group * SUB, SUB), pl.ds(t * LANES, LANES)] = parts[t]
    store = pltpu.make_async_copy(natural, fine_hbm, local.at[5])
    store.start()

    @pl.when(has_before)
    def _():
        for plane, j in each_slab():
            end[plane, j] = restricted(plane, j, SUB, coarse_count)

        @pl.when(jnp.logical_not(has_up))
        def _():
            above_in[...] = jnp.zeros_like(above_in)

        @pl.when(jnp.logical_not(has_down))
        def _():
            below_in[...] = jnp.zeros_like(below_in)

        @pl.when(has_up)
        def _():
            for copy in to_below:
                copy.wait_recv()

        @pl.when(has_down)
        def _():
            for copy in to_above:
                copy.wait_recv()

        at = lax.broadcasted_iota(jnp.int32, (SUB, LANES), 0)
        for plane, j in each_slab():
            around = jnp.where(
                at < HALO[plane],
                below_in[plane, j],
                jnp.where(
                    at >= SUB - HALO[plane],
                    pltpu.roll(above_in[plane, j], SUB - HALO[plane], 0),
                    0.0,
                ),
            )
            c_state[plane, j, pl.ds(coarse_count, SUB), :] = around - far_start[plane, j]
        to_own.wait_recv()
        for plane, j in each_slab():
            c_state[plane, j, pl.ds(0, coarse_count), :] = arrived[plane, j] - start[plane, j]
        coarse_inside = mask(coarse_count + SUB, 0, total_rows // 2, tile * coarse_count)
        wave(
            c_state, c_height, c_held, coarse_rows, coarse_weights, half, tiles,
            COARSE_STEP / (2.0 * COARSE_SPACING), coarse_inside,
        )
        for plane, j in each_slab():
            leave(plane, j, c_state[plane, j, pl.ds(0, coarse_count), :] + end[plane, j])
        launch()
        for plane, j in each_slab():
            gain_ref[plane, j] = c_state[plane, j, pl.ds(0, coarse_count), :]

    store.wait()

    @pl.when(has_down)
    def _():
        main_down.wait_send()
        edge_down.wait_send()

    @pl.when(has_up)
    def _():
        main_up.wait_send()
        edge_up.wait_send()

    @pl.when(has_after & has_up)
    def _():
        for copy in to_above:
            copy.wait_send()

    @pl.when(has_after & has_down)
    def _():
        for copy in to_below:
            copy.wait_send()

    @pl.when(has_after)
    def _():
        to_own.wait_send()


def finish(fine_ref, gain_ref, out_hbm, spread, result, done):
    planes, tiles, row_count, _ = spread.shape
    stores = []
    for plane in range(planes):
        parts = relaid([gain_ref[plane, j // 2] for j in range(tiles)])
        for t in range(tiles):
            for r in range(2):
                spread[plane, t, pl.ds(r, row_count // 2, stride=2), :] = parts[t]
        for t in range(tiles):
            columns = pl.ds(t * LANES, LANES)
            result[plane, :, columns] = fine_ref[plane, :, columns] + spread[plane, t]
        stores.append(
            pltpu.make_async_copy(result.at[plane], out_hbm.at[plane], done.at[plane])
        )
        stores[-1].start()
    for store in stores:
        store.wait()


def per_device(tile_count, slices, start_states):
    fields = start_states[0]
    planes, row_count, columns = fields.shape
    tiles = columns // LANES
    half = tiles // 2
    fine = line_tables(tiles, tiles, 1.0, columns, FINE_SPACING, FINE_STEP)
    coarse = line_tables(half, tiles, 2.0, columns, COARSE_SPACING, COARSE_STEP)
    fine_count = row_count + 3 * SUB
    coarse_count = row_count // 2
    f32 = jnp.float32
    slab = pltpu.VMEM((planes, half, coarse_count, LANES), f32)
    fine_end, gain = pl.pallas_call(
        functools.partial(kernel, tile_count, slices),
        out_shape=[
            jax.ShapeDtypeStruct(fields.shape, f32),
            jax.ShapeDtypeStruct((planes, half, coarse_count, LANES), f32),
        ],
        in_specs=[pl.BlockSpec(memory_space=pl.ANY)] * 5,
        out_specs=[
            pl.BlockSpec(memory_space=pl.ANY),
            pl.BlockSpec(memory_space=pltpu.VMEM),
        ],
        scratch_shapes=[pltpu.VMEM(fields.shape, f32)] * 2
        + [pltpu.VMEM(a.shape, f32) for a in fine + coarse]
        + [pltpu.VMEM((planes, SUB, columns), f32)] * 2
        + [pltpu.VMEM((SUB, columns), f32)] * 3
        + [
            pltpu.VMEM((planes, tiles, fine_count, LANES), f32),
            pltpu.VMEM((tiles, fine_count, LANES), f32),
            pltpu.VMEM((tiles, 2 * fine_count, LANES), f32),
            pltpu.VMEM((planes, half, 2 * coarse_count, LANES), f32),
            pltpu.VMEM((half, 2 * coarse_count, LANES), f32),
            pltpu.VMEM((half, 4 * coarse_count, LANES), f32),
        ]
        + [slab] * 8
        + [
            pltpu.SemaphoreType.DMA((6,)),
            pltpu.SemaphoreType.DMA((9,)),
            pltpu.SemaphoreType.DMA((9,)),
        ],
        compiler_params=pltpu.CompilerParams(collective_id=0, has_side_effects=True),
    )(fields, *[jnp.asarray(a) for a in fine + coarse])
    out = pl.pallas_call(
        finish,
        out_shape=jax.ShapeDtypeStruct(fields.shape, f32),
        in_specs=[pl.BlockSpec(memory_space=pltpu.VMEM)] * 2,
        out_specs=pl.BlockSpec(memory_space=pl.ANY),
        scratch_shapes=[
            pltpu.VMEM((planes, tiles, row_count, LANES), f32),
            pltpu.VMEM(fields.shape, f32),
            pltpu.SemaphoreType.DMA((planes,)),
        ],
    )(fine_end, gain)
    return out[None]


def solution(mesh):
    spec = P("cuts", None, "tile", None)
    body = functools.partial(per_device, mesh.shape["tile"], mesh.shape["cuts"])
    return jax.shard_map(body, mesh=mesh, in_specs=(spec,), out_specs=spec, check_vma=False)
```
